32 devices in a mesh: groups: 2 (over y), mesh: 4 (over z), edge: 4 (over x, core).
Axes of the slice: x: 2, y: 2, z: 4, core: 2. Of those that a mesh axis runs over, the one named last changes fastest.
Arguments:
- grid_input: bfloat16 [16384, 474], P(('groups', 'mesh', 'edge')), parts along dimension 0, may hold values from -6 to 6
- mesh_position: bfloat16 [3, 256], P(None, ('mesh', 'edge')), may hold values from -1 to 1
- encoder_senders: int32 [32768], P(('mesh', 'edge')), may hold values from 0 to 8191, as said below
- encoder_receivers: int32 [32768], P(('mesh', 'edge')), may hold values from 0 to 255, as said below
- encoder_features: bfloat16 [4, 32768], P(None, ('mesh', 'edge')), may hold values from -6 to 6
- encoder_counts: int32 [16], P(('mesh', 'edge')), may hold values from 1 to 16, as said below
- mesh_senders: int32 [4096], P(('mesh', 'edge')), may hold values from 0 to 255, as said below
- mesh_receivers: int32 [4096], P(('mesh', 'edge')), may hold values from 0 to 255, as said below
- mesh_features: bfloat16 [4, 4096], P(None, ('mesh', 'edge')), may hold values from -6 to 6
- cotangent: bfloat16 [512, 512], P(('groups', 'mesh', 'edge')), parts along dimension 0, may hold values from -6 to 6
- grid_first: bfloat16 [474, 512], replicated, may hold values from -0.25 to 0.25
- grid_second: bfloat16 [512, 512], replicated, may hold values from -0.25 to 0.25
- encoder_inner: bfloat16 [512, 512], replicated, may hold values from -0.25 to 0.25
- encoder_geometry: bfloat16 [4, 512], replicated, may hold values from -3 to 3
- encoder_outer: bfloat16 [512, 512], replicated, may hold values from -0.25 to 0.25
- node_first: bfloat16 [512, 512], replicated, may hold values from -0.25 to 0.25
- node_position: bfloat16 [3, 512], replicated, may hold values from -3.5 to 3.5
- node_second: bfloat16 [512, 512], replicated, may hold values from -0.25 to 0.25
- edge_sender: bfloat16 [512, 512], replicated, may hold values from -0.25 to 0.25
- edge_receiver: bfloat16 [512, 512], replicated, may hold values from -0.25 to 0.25
- edge_geometry: bfloat16 [4, 512], replicated, may hold values from -3 to 3
- edge_outer: bfloat16 [512, 512], replicated, may hold values from -0.25 to 0.25
- update_message: bfloat16 [512, 512], replicated, may hold values from -0.25 to 0.25
- update_state: bfloat16 [512, 512], replicated, may hold values from -0.25 to 0.25
- update_outer: bfloat16 [512, 512], replicated, may hold values from -0.25 to 0.25
Outputs:
- mesh_output: bfloat16 [512, 512], P(('groups', 'mesh', 'edge')), parts along dimension 0
- mesh_gradient: float32 [512, 512], P(('groups', 'mesh', 'edge')), parts along dimension 0
The draws below stay inside these ranges and needn't reach their ends.
There are 2 independent parts, one for each index of `groups`. The reference program is written for one: setup_inputs(seed, part) draws one part's arguments, and reference() takes and returns one part's arrays. A program takes and returns all parts, laid end to end along the dimension named above; an argument that names none is the same for every part. Nothing has to cross between parts.
Inputs may be any that keep to these rules, and one draw needn't show every extreme that they name: `encoder_senders`: an encoder edge slot of a device with mesh index b has its sender in band b: from b * 2048 to (b + 1) * 2048 - 1. `encoder_receivers`: an encoder edge slot of a device with mesh index b has its receiver among the mesh nodes b * 64 to (b + 1) * 64 - 1. `encoder_counts`: slots in blocks at or beyond a device's count carry no edge. For every mesh index, one device of the edge axis has all 16 blocks live. `mesh_receivers`: A multimesh edge of a device with mesh index b has its receiver among the mesh nodes b * 64 to (b + 1) * 64 - 1. `mesh_senders`: A multimesh edge of a device with mesh index b has its sender either among the mesh nodes b * 64 to (b + 1) * 64 - 1, or at a node n with n mod 16 below 4.
All inputs are finite; a program needn't handle non-finite values.
Results may differ from the reference program's by a relative error of at most 0.039.
Values may be sent and summed in bfloat16 or wider, within the bound.
No kernel may reach another device: no remote copies, remote signals or barrier semaphores. Data moves between devices by JAX's collectives and lax.ppermute only.
A program may use at most 128 MiB of HBM per device.

```python
import jax
import jax.numpy as jnp
from jax import lax

CHANNELS = 474
LATENT = 512
MESH_DEV = 16
COARSE_DEV = 4
BLOCK = 128
G2M_BLOCKS = 16
M2M_BLOCKS = 2
OWNERS = 16
GRID = 8192
BAND = 2048
MESH = 256
SHARD = 64
G2M_EDGES = 32768
M2M_EDGES = 4096
N_MESH = 4
N_EDGE = 4


def slot_band(total, per_device):
    return jnp.arange(total, dtype=jnp.int32) // per_device // N_EDGE


def draw_encoder_senders(key, part):
    band_number = slot_band(G2M_EDGES, G2M_BLOCKS * BLOCK)
    offsets = jax.random.randint(jax.random.fold_in(key, 11), (G2M_EDGES,), 0, BAND)
    return (band_number * BAND + offsets).astype(jnp.int32)


def draw_encoder_receivers(key, part):
    band_number = slot_band(G2M_EDGES, G2M_BLOCKS * BLOCK)
    offsets = jax.random.randint(jax.random.fold_in(key, 12), (G2M_EDGES,), 0, SHARD)
    return (band_number * SHARD + offsets).astype(jnp.int32)


def draw_encoder_counts(key, part):
    busiest = jax.random.randint(jax.random.fold_in(key, 13), (N_MESH,), 0, N_EDGE)
    lowest = max(G2M_BLOCKS // 4, 1)
    highest = max(3 * G2M_BLOCKS // 8, lowest)
    lighter = jax.random.randint(jax.random.fold_in(key, 14), (OWNERS,), lowest, highest + 1)
    devices = jnp.arange(OWNERS, dtype=jnp.int32)
    heavy = devices % N_EDGE == busiest[devices // N_EDGE]
    return jnp.where(heavy, G2M_BLOCKS, lighter).astype(jnp.int32)


def draw_mesh_receivers(key, part):
    band_number = slot_band(M2M_EDGES, M2M_BLOCKS * BLOCK)
    offsets = jax.random.randint(jax.random.fold_in(key, 15), (M2M_EDGES,), 0, SHARD)
    return (band_number * SHARD + offsets).astype(jnp.int32)


def draw_mesh_senders(key, part):
    band_number = slot_band(M2M_EDGES, M2M_BLOCKS * BLOCK)
    nearby = band_number * SHARD + jax.random.randint(jax.random.fold_in(key, 16), (M2M_EDGES,), 0, SHARD)
    owners = jax.random.randint(jax.random.fold_in(key, 17), (M2M_EDGES,), 0, OWNERS)
    coarse = owners * MESH_DEV + jax.random.randint(jax.random.fold_in(key, 18), (M2M_EDGES,), 0, COARSE_DEV)
    faraway = jax.random.randint(jax.random.fold_in(key, 19), (M2M_EDGES,), 0, 4) == 0
    return jnp.where(faraway, coarse, nearby).astype(jnp.int32)


def block_scale(rng, shape, pieces, least, high):
    loudness = 1.0
    for position, blocks in pieces:
        draws = jax.random.uniform(jax.random.fold_in(jax.random.fold_in(rng, 6), position), (blocks,), jnp.float32, least / len(pieces), high / len(pieces))
        loudness = loudness * jnp.repeat(jnp.exp(draws), shape[position] // blocks).reshape((-1,) + (1,) * (len(shape) - 1 - position))
    return loudness


def gaussian(rng, dims, scale, most, shards=(), kind=jnp.bfloat16):
    entries = scale * jax.random.normal(rng, dims, jnp.float32)
    if shards:
        entries = entries * block_scale(rng, dims, shards, -0.22, 0.18)
    return jnp.clip(entries, -most, most).astype(kind)


def setup_inputs(seed: int = 0, part: int = 0) -> dict:
    key_of = jax.random.split(jax.random.key(seed), 26)
    part_keys = jax.random.split(jax.random.fold_in(key_of[25], part), 26)
    return {
        "grid_input": gaussian(part_keys[0], (GRID, CHANNELS), 1.0, 6.0, ((0, 16),)),
        "mesh_position": jnp.clip(jax.random.uniform(key_of[1], (3, MESH), jnp.float32, -1.0, 1.0) * block_scale(key_of[1], (3, MESH), ((1, 16),), -0.4, 0.0), -1.0, 1.0).astype(jnp.bfloat16),
        "encoder_senders": draw_encoder_senders(jax.random.fold_in(key_of[25], 71), part),
        "encoder_receivers": draw_encoder_receivers(jax.random.fold_in(key_of[25], 71), part),
        "encoder_features": gaussian(key_of[4], (4, G2M_EDGES), 1.0, 6.0, ((1, 16),)),
        "encoder_counts": draw_encoder_counts(jax.random.fold_in(key_of[25], 71), part),
        "mesh_senders": draw_mesh_senders(jax.random.fold_in(key_of[25], 71), part),
        "mesh_receivers": draw_mesh_receivers(jax.random.fold_in(key_of[25], 71), part),
        "mesh_features": gaussian(key_of[8], (4, M2M_EDGES), 1.0, 6.0, ((1, 16),)),
        "cotangent": gaussian(part_keys[9], (MESH, LATENT), 1.0, 6.0, ((0, 16),)),
        "grid_first": gaussian(key_of[10], (CHANNELS, LATENT), CHANNELS ** -0.5, 0.25),
        "grid_second": gaussian(key_of[11], (LATENT, LATENT), LATENT ** -0.5, 0.25),
        "encoder_inner": gaussian(key_of[12], (LATENT, LATENT), LATENT ** -0.5, 0.25),
        "encoder_geometry": gaussian(key_of[13], (4, LATENT), 4 ** -0.5, 3.0),
        "encoder_outer": gaussian(key_of[14], (LATENT, LATENT), LATENT ** -0.5, 0.25),
        "node_first": gaussian(key_of[15], (LATENT, LATENT), LATENT ** -0.5, 0.25),
        "node_position": gaussian(key_of[16], (3, LATENT), 3 ** -0.5, 3.5),
        "node_second": gaussian(key_of[17], (LATENT, LATENT), LATENT ** -0.5, 0.25),
        "edge_sender": gaussian(key_of[18], (LATENT, LATENT), LATENT ** -0.5, 0.25),
        "edge_receiver": gaussian(key_of[19], (LATENT, LATENT), LATENT ** -0.5, 0.25),
        "edge_geometry": gaussian(key_of[20], (4, LATENT), 4 ** -0.5, 3.0),
        "edge_outer": gaussian(key_of[21], (LATENT, LATENT), LATENT ** -0.5, 0.25),
        "update_message": gaussian(key_of[22], (LATENT, LATENT), LATENT ** -0.5, 0.25),
        "update_state": gaussian(key_of[23], (LATENT, LATENT), LATENT ** -0.5, 0.25),
        "update_outer": gaussian(key_of[24], (LATENT, LATENT), LATENT ** -0.5, 0.25),
    }


def product(left, right):
    return jnp.dot(left, right, preferred_element_type=jnp.float32)

def layer_norm(values):
    centred = values - lax.optimization_barrier(jnp.mean(values, axis=-1, keepdims=True))
    variance = lax.optimization_barrier(jnp.mean(centred * centred, axis=-1, keepdims=True))
    return centred * lax.rsqrt(variance + 1e-05)

def silu_grad(values):
    sigma = jax.nn.sigmoid(values)
    return sigma * (1.0 + values * (1.0 - sigma))

def reference(grid_input, mesh_position, encoder_senders, encoder_receivers, encoder_features, encoder_counts, mesh_senders, mesh_receivers, mesh_features, cotangent, grid_first, grid_second, encoder_inner, encoder_geometry, encoder_outer, node_first, node_position, node_second, edge_sender, edge_receiver, edge_geometry, edge_outer, update_message, update_state, update_outer):
    grid_hidden = jax.nn.silu(product(grid_input, grid_first)).astype(jnp.bfloat16)
    grid_latent = layer_norm(product(grid_hidden, grid_second)).astype(jnp.bfloat16)
    per_device = G2M_BLOCKS * BLOCK
    slots = jnp.arange(G2M_EDGES, dtype=jnp.int32)
    owner = slots // per_device
    block_number = slots % per_device // BLOCK
    live = (block_number < encoder_counts[owner]).astype(jnp.float32)
    enc_pre = product(grid_latent[encoder_senders], encoder_inner) + product(encoder_features.T, encoder_geometry)
    enc_act = jax.nn.silu(enc_pre).astype(jnp.bfloat16)
    enc_message = product(enc_act, encoder_outer) * live[:, None]
    enc_sum = jnp.zeros((MESH, LATENT), jnp.float32).at[encoder_receivers].add(enc_message)
    node_hidden = jax.nn.silu(product(enc_sum.astype(jnp.bfloat16), node_first) + product(mesh_position.T, node_position)).astype(jnp.bfloat16)
    mesh_latent = layer_norm(product(node_hidden, node_second)).astype(jnp.bfloat16)
    proc_pre = product(mesh_latent[mesh_senders], edge_sender) + product(mesh_latent[mesh_receivers], edge_receiver) + product(mesh_features.T, edge_geometry)
    proc_act = jax.nn.silu(proc_pre).astype(jnp.bfloat16)
    proc_message = product(proc_act, edge_outer)
    proc_sum = jnp.zeros((MESH, LATENT), jnp.float32).at[mesh_receivers].add(proc_message).astype(jnp.bfloat16)
    update_pre = product(proc_sum, update_message) + product(mesh_latent, update_state)
    update_act = jax.nn.silu(update_pre).astype(jnp.bfloat16)
    mesh_output = (mesh_latent.astype(jnp.float32) + product(update_act, update_outer)).astype(jnp.bfloat16)
    grad_pre = (product(cotangent, update_outer.T) * silu_grad(update_pre)).astype(jnp.bfloat16)
    grad_sum = product(grad_pre, update_message.T).astype(jnp.bfloat16)
    grad_node = cotangent.astype(jnp.float32) + product(grad_pre, update_state.T)
    grad_edge = (product(grad_sum[mesh_receivers], edge_outer.T) * silu_grad(proc_pre)).astype(jnp.bfloat16)
    mesh_gradient = grad_node.at[mesh_senders].add(product(grad_edge, edge_sender.T))
    mesh_gradient = mesh_gradient.at[mesh_receivers].add(product(grad_edge, edge_receiver.T))
    return (mesh_output, mesh_gradient)
```

```python
import functools

import jax
import jax.numpy as jnp
from jax import lax
from jax.experimental import pallas as pl
from jax.experimental.pallas import tpu as pltpu
from jax.sharding import PartitionSpec as P

BLOCK = 128
PERIOD = 16
COARSE = 4
RADIX = 256
BF = jnp.bfloat16
F32 = jnp.float32
IN_VMEM = pl.BlockSpec(memory_space=pltpu.VMEM)
IN_SMEM = pl.BlockSpec(memory_space=pltpu.SMEM)


def nn(left, right):
    return jnp.dot(left, right, preferred_element_type=F32)


def nt(left, right):
    return lax.dot_general(left, right, (((1,), (1,)), ((), ())), preferred_element_type=F32)


def tn(left, right):
    return lax.dot_general(left, right, (((0,), (0,)), ((), ())), preferred_element_type=F32)


def silu(values):
    half = 0.5 * values
    return half + half * jnp.tanh(half)


def silu_grad(values):
    half = 0.5 * values
    bend = jnp.tanh(half)
    return 0.5 * (1.0 + bend) * (1.0 + half * (1.0 - bend))


def layer_norm(values):
    centred = values - jnp.mean(values, axis=-1, keepdims=True)
    variance = jnp.mean(centred * centred, axis=-1, keepdims=True)
    return centred * lax.rsqrt(variance + 1e-05)


def one_hot(rows, index):
    places = lax.broadcasted_iota(jnp.int32, (rows, index.shape[1]), 0)
    return (places == index).astype(F32).astype(BF)


def shift_of(size):
    assert size & (size - 1) == 0
    return size.bit_length() - 1


def split(values):
    high = lax.shift_right_logical(values, shift_of(RADIX))
    return high.astype(F32), (values - high * RADIX).astype(F32)


def join(rows):
    return (rows[0:1] * RADIX + rows[1:2]).astype(jnp.int32)


def geometry_rows(weights, height):
    count, width = weights.shape
    return jnp.concatenate(
        [
            jnp.zeros((3, width), F32),
            0.5 * weights.astype(F32),
            jnp.zeros((height - 3 - count, width), F32),
        ],
        axis=0,
    )


def pack_kernel(
    sizes, count_ref, send_ref, recv_ref, feat_ref, msend_ref, mrecv_ref, mfeat_ref, pos_ref, cot_ref, out_ref, work_ref
):
    band, half, width, edges = sizes["band"], sizes["half"], sizes["width"], sizes["edges"]
    shard = sizes["shard"]
    b = lax.axis_index("mesh")
    live = count_ref[0] * BLOCK
    work_ref[...] = jnp.zeros_like(work_ref)
    senders = send_ref[...] - b * band
    high, low = split(senders)
    receivers = (recv_ref[...] - b * shard).astype(F32)
    features = feat_ref[...].astype(F32)
    alive = (lax.broadcasted_iota(jnp.int32, senders.shape, 1) < live).astype(F32)
    for part in range(2):
        lanes = slice(part * half, (part + 1) * half)
        base = part * 8
        work_ref[base : base + 1, 0:half] = high[:, lanes]
        work_ref[base + 1 : base + 2, 0:half] = low[:, lanes]
        work_ref[base + 2 : base + 3, 0:half] = receivers[:, lanes]
        work_ref[base + 3 : base + 7, 0:half] = features[:, lanes]
        work_ref[base + 7 : base + 8, 0:half] = alive[:, lanes]
    work_ref[:, half : half + width] = cot_ref[...].astype(F32)
    node = msend_ref[...]
    local = node - b * shard
    near = (local >= 0) & (local < shard)
    owner = lax.shift_right_logical(node, shift_of(PERIOD))
    far_band = lax.shift_right_logical(owner, shift_of(sizes["n_edge"]))
    step = lax.bitwise_xor(far_band, b)
    seat = lax.bitwise_and(owner, sizes["n_edge"] - 1)
    far = shard + ((step - 1) * sizes["n_edge"] + seat) * COARSE + lax.bitwise_and(node, PERIOD - 1)
    high, low = split(jnp.where(near, local, far))
    start = half + width
    work_ref[0:1, start : start + edges] = high
    work_ref[1:2, start : start + edges] = low
    work_ref[2:3, start : start + edges] = (mrecv_ref[...] - b * shard).astype(F32)
    work_ref[3:7, start : start + edges] = mfeat_ref[...].astype(F32)
    work_ref[8:11, start : start + sizes["rows"]] = pos_ref[...].astype(F32)
    out_ref[...] = work_ref[...].astype(BF)


def grid_kernel(grid_ref, first_ref, second_ref, inner_ref, geom_ref, table_ref, geom_out):
    hidden = silu(nn(grid_ref[...], first_ref[...])).astype(BF)
    latent = layer_norm(nn(hidden, second_ref[...])).astype(BF)
    table_ref[...] = (0.5 * nn(latent, inner_ref[...])).T.astype(BF)
    geom_out[...] = geometry_rows(geom_ref[...], 8).T.astype(BF)


def encode_kernel(sizes, chunk, *refs):
    n_edge, half, shard = sizes["n_edge"], sizes["half"], sizes["shard"]
    packs = refs[:n_edge]
    table_ref, geom_ref, out_ref, list_ref, acc_ref = refs[n_edge:]
    own = table_ref.shape[1]
    e = lax.axis_index("edge")
    per_half = half // chunk
    counts = []
    for d in range(n_edge):
        total = jnp.float32(0)
        for j in range(per_half):
            rows = packs[d][:, j * chunk : (j + 1) * chunk].astype(F32)
            list_ref[2 * per_half * d + j] = rows[0:8]
            list_ref[2 * per_half * d + per_half + j] = rows[8:16]
            total = total + jnp.sum(rows[7:8]) + jnp.sum(rows[15:16])
        counts.append((total.astype(jnp.int32) + (chunk - 1)) // chunk)
    acc_ref[...] = jnp.zeros_like(acc_ref)

    def body(step, carry):
        place = step
        before = jnp.int32(0)
        for d in range(n_edge):
            after = before + counts[d]
            inside = (step >= before) & (step < after)
            place = jnp.where(inside, 2 * per_half * d + step - before, place)
            before = after
        rows = list_ref[place]
        sender = join(rows) - e * own
        mine = (sender >= 0) & (sender < own) & (rows[7:8] > 0)
        receiver = jnp.where(mine, rows[2:3].astype(jnp.int32), -1)
        half_pre = nn(table_ref[...], one_hot(own, sender)) + nn(geom_ref[...], rows.astype(BF))
        act = (half_pre + half_pre * jnp.tanh(half_pre)).astype(BF)
        acc_ref[...] += nt(one_hot(shard, receiver), act)
        return carry

    lax.fori_loop(0, sum(counts), body, 0)
    out_ref[...] = acc_ref[...].astype(BF)


def node_kernel(sizes, parts_count, *refs):
    n_edge, rows, start = sizes["n_edge"], sizes["rows"], sizes["half"] + sizes["width"]
    packs, refs = refs[:n_edge], refs[n_edge:]
    parts, refs = refs[:parts_count], refs[parts_count:]
    outer_ref, first_ref, posw_ref, second_ref, latent_ref, coarse_ref, pos_ref, coarse_work = refs
    e = lax.axis_index("edge")
    posw = jnp.concatenate(
        [posw_ref[...].astype(F32), jnp.zeros((8 - posw_ref.shape[0], posw_ref.shape[1]), F32)], axis=0
    ).astype(BF)
    for d in range(n_edge):
        block = packs[d][:, start : start + 128].astype(F32)[8:16].T[0:rows].astype(BF)
        seat = pl.multiple_of(lax.bitwise_xor(e, d) * rows, rows)
        pos_ref[pl.ds(seat, rows), :] = nn(block, posw)
    total = parts[0][...].astype(F32)
    for part in parts[1:]:
        total = total + part[...].astype(F32)
    enc_sum = nn(total.astype(BF), outer_ref[...]).astype(BF)
    hidden = silu(nn(enc_sum, first_ref[...]) + pos_ref[...]).astype(BF)
    latent = layer_norm(nn(hidden, second_ref[...]))
    latent_ref[...] = latent.astype(BF)
    for d in range(n_edge):
        coarse_work[d * COARSE : (d + 1) * COARSE] = latent[d * rows : d * rows + COARSE]
    coarse_ref[...] = coarse_work[...].astype(BF)


def process_kernel(sizes, *refs):
    n_edge, n_mesh, rows, shard = sizes["n_edge"], sizes["n_mesh"], sizes["rows"], sizes["shard"]
    half, width, edges = sizes["half"], sizes["width"], sizes["edges"]
    packs, refs = refs[:n_edge], refs[n_edge:]
    latent_ref, refs = refs[0], refs[1:]
    coarse, refs = refs[: n_mesh - 1], refs[n_mesh - 1 :]
    send_w, recv_w, geom_w, outer_w, message_w, state_w, update_w = refs[:7]
    refs = refs[7:]
    far_out, refs = refs[: n_mesh - 1], refs[n_mesh - 1 :]
    keep_ref, cot_ref, slope_ref, stack_ref = refs
    e = lax.axis_index("edge")
    start = half + width
    lists = []
    for d in range(n_edge):
        lists.append(packs[d][:, start : start + edges])
        seat = pl.multiple_of(lax.bitwise_xor(e, d) * rows, rows)
        cot_ref[pl.ds(seat, rows), :] = packs[d][:, half : half + width]
    lists = jnp.concatenate(lists, axis=1)
    values = lists.astype(F32)[0:8]
    sender = join(values)
    receiver = values[2:3].astype(jnp.int32)
    latent = latent_ref[...]
    table = jnp.concatenate([latent] + [c[...] for c in coarse], axis=0)
    near_far = table.shape[0]
    products = jnp.concatenate(
        [
            (0.5 * nn(table, send_w[...])).astype(BF),
            (0.5 * nn(latent, recv_w[...])).astype(BF),
            geometry_rows(geom_w[...], 16).astype(BF),
        ],
        axis=0,
    )
    pick_receiver = one_hot(shard, receiver)
    picks = jnp.concatenate([one_hot(near_far, sender), pick_receiver, lists], axis=0)
    half_pre = tn(products, picks)
    bend = jnp.tanh(half_pre)
    act = (half_pre + half_pre * bend).astype(BF)
    slope_ref[...] = 0.5 * (1.0 + bend) * (1.0 + half_pre * (1.0 - bend))
    proc_sum = nn(nt(pick_receiver, act).astype(BF), outer_w[...]).astype(BF)
    update_pre = nn(proc_sum, message_w[...]) + nn(latent, state_w[...])
    update_act = silu(update_pre).astype(BF)
    grad_pre = (nt(cot_ref[...], update_w[...]) * silu_grad(update_pre)).astype(BF)
    grad_sum = nt(grad_pre, message_w[...]).astype(BF)
    grad_act = nt(grad_sum, outer_w[...]).astype(BF)
    grad_edge = (tn(grad_act, pick_receiver) * slope_ref[...]).astype(BF)
    far = sender - shard
    far_seat = lax.bitwise_and(lax.shift_right_logical(far, shift_of(COARSE)), n_edge - 1)
    far_row = lax.shift_right_logical(far, shift_of(COARSE * n_edge)) * COARSE + lax.bitwise_and(far, COARSE - 1)
    far_row = jnp.where((far >= 0) & (far_seat == e), far_row, -1)
    far_height = -(-(n_mesh - 1) * COARSE // 16) * 16
    near_row = jnp.where(far < 0, sender - e * rows, -1)
    spread = jnp.concatenate(
        [one_hot(far_height, far_row), one_hot(rows, near_row), one_hot(rows, receiver - e * rows)], axis=0
    )
    sums = nt(spread, grad_edge).astype(BF)
    returned = nt(sums[0:far_height], send_w[...])
    for m in range(n_mesh - 1):
        far_out[m][...] = returned[m * COARSE : (m + 1) * COARSE]
    stack_ref[0] = latent
    stack_ref[1] = update_act
    stack_ref[2] = grad_pre
    stack_ref[3] = cot_ref[...]
    seat = pl.multiple_of(e * rows, rows)
    for k in range(4):
        keep_ref[k] = stack_ref[k, pl.ds(seat, rows), :]
    keep_ref[4] = sums[far_height : far_height + rows]
    keep_ref[5] = sums[far_height + rows : far_height + 2 * rows]


def finish_kernel(keep_ref, send_w, recv_w, state_w, update_w, out_ref, base_ref):
    out_ref[...] = (keep_ref[0].astype(F32) + nn(keep_ref[1], update_w[...])).astype(BF)
    base_ref[...] = (
        keep_ref[3].astype(F32)
        + nt(keep_ref[2], state_w[...])
        + nt(keep_ref[4], send_w[...])
        + nt(keep_ref[5], recv_w[...])
    )


def call(kernel, name, outs, scratch=(), specs=None):
    def run(*args):
        return pl.pallas_call(
            kernel,
            name=name,
            out_shape=[jax.ShapeDtypeStruct(shape, dtype) for shape, dtype in outs],
            in_specs=specs or [IN_VMEM] * len(args),
            out_specs=[IN_VMEM] * len(outs),
            scratch_shapes=list(scratch),
        )(*args)

    return run


def partner(value, axis, size, step):
    return lax.ppermute(value, axis, [(i, i ^ step) for i in range(size)])


def shards(
    grid_input,
    mesh_position,
    encoder_senders,
    encoder_receivers,
    encoder_features,
    encoder_counts,
    mesh_senders,
    mesh_receivers,
    mesh_features,
    cotangent,
    grid_first,
    grid_second,
    encoder_inner,
    encoder_geometry,
    encoder_outer,
    node_first,
    node_position,
    node_second,
    edge_sender,
    edge_receiver,
    edge_geometry,
    edge_outer,
    update_message,
    update_state,
    update_outer,
):
    n_edge, n_mesh = lax.axis_size("edge"), lax.axis_size("mesh")
    own, width = grid_input.shape[0], grid_second.shape[1]
    rows, slots, edges = mesh_position.shape[1], encoder_senders.shape[0], mesh_senders.shape[0]
    shard, half = rows * n_edge, encoder_senders.shape[0] // 2
    assert rows == PERIOD and n_edge & (n_edge - 1) == 0 and n_mesh & (n_mesh - 1) == 0
    sizes = dict(
        n_edge=n_edge, n_mesh=n_mesh, rows=rows, shard=shard, half=half, width=width, edges=edges, band=own * n_edge
    )
    lanes = half + width + edges
    (pack,) = call(
        functools.partial(pack_kernel, sizes),
        "pack",
        [((16, lanes), BF)],
        [pltpu.VMEM((16, lanes), F32)],
        [IN_SMEM] + [IN_VMEM] * 8,
    )(
        encoder_counts,
        encoder_senders.reshape(1, slots),
        encoder_receivers.reshape(1, slots),
        encoder_features,
        mesh_senders.reshape(1, edges),
        mesh_receivers.reshape(1, edges),
        mesh_features,
        mesh_position,
        cotangent,
    )
    packs = [pack] + [partner(pack, "edge", n_edge, m) for m in range(1, n_edge)]
    table, geometry = call(grid_kernel, "grid", [((width, own), BF), ((width, 8), BF)])(
        grid_input, grid_first, grid_second, encoder_inner, encoder_geometry
    )
    chunk = min(512, half)
    (partial,) = call(
        functools.partial(encode_kernel, sizes, chunk),
        "encode",
        [((shard, width), BF)],
        [pltpu.VMEM((n_edge * slots // chunk, 8, chunk), F32), pltpu.VMEM((shard, width), F32)],
    )(*packs, table, geometry)
    parts = [partial] + [partner(partial, "edge", n_edge, m) for m in range(1, n_edge)]
    latent, coarse = call(
        functools.partial(node_kernel, sizes, len(parts)),
        "node",
        [((shard, width), BF), ((n_edge * COARSE, width), BF)],
        [pltpu.VMEM((shard, width), F32), pltpu.VMEM((n_edge * COARSE, width), F32)],
    )(*packs, *parts, encoder_outer, node_first, node_position, node_second)
    others = [partner(coarse, "mesh", n_mesh, m) for m in range(1, n_mesh)]
    *far, keep = call(
        functools.partial(process_kernel, sizes),
        "process",
        [((COARSE, width), F32)] * (n_mesh - 1) + [((6, rows, width), BF)],
        [
            pltpu.VMEM((shard, width), BF),
            pltpu.VMEM((width, edges * n_edge), F32),
            pltpu.VMEM((4, shard, width), BF),
        ],
    )(
        *packs,
        latent,
        *others,
        edge_sender,
        edge_receiver,
        edge_geometry,
        edge_outer,
        update_message,
        update_state,
        update_outer,
    )
    returned = [partner(far[m - 1], "mesh", n_mesh, m) for m in range(1, n_mesh)]
    output, base = call(finish_kernel, "finish", [((rows, width), BF), ((rows, width), F32)])(
        keep, edge_sender, edge_receiver, update_state, update_outer
    )
    coarse_part = functools.reduce(jnp.add, returned)
    gradient = jnp.concatenate([base[:COARSE] + coarse_part, base[COARSE:]], axis=0)
    return (output, gradient)


def solution(mesh):
    nodes = P(("groups", "mesh", "edge"), None)
    flat = P(("mesh", "edge"))
    lanes = P(None, ("mesh", "edge"))
    in_specs = (nodes, lanes, flat, flat, lanes, flat, flat, flat, lanes, nodes) + (P(),) * 15
    return jax.shard_map(shards, mesh=mesh, in_specs=in_specs, out_specs=(nodes, nodes), check_vma=False)
```

```python
import functools

import jax
import jax.numpy as jnp
from jax import lax
from jax.experimental import pallas as pl
from jax.experimental.pallas import tpu as pltpu
from jax.sharding import PartitionSpec as P

BLOCK = 128
PERIOD = 16
COARSE = 4
RADIX = 256
BF = jnp.bfloat16
F32 = jnp.float32
IN_VMEM = pl.BlockSpec(memory_space=pltpu.VMEM)
IN_SMEM = pl.BlockSpec(memory_space=pltpu.SMEM)


def nn(left, right):
    return jnp.dot(left, right, preferred_element_type=F32)


def nt(left, right):
    return lax.dot_general(left, right, (((1,), (1,)), ((), ())), preferred_element_type=F32)


def tn(left, right):
    return lax.dot_general(left, right, (((0,), (0,)), ((), ())), preferred_element_type=F32)


def silu(values):
    half = 0.5 * values
    return half + half * jnp.tanh(half)


def silu_grad(values):
    half = 0.5 * values
    bend = jnp.tanh(half)
    return 0.5 * (1.0 + bend) * (1.0 + half * (1.0 - bend))


def layer_norm(values):
    centred = values - jnp.mean(values, axis=-1, keepdims=True)
    variance = jnp.mean(centred * centred, axis=-1, keepdims=True)
    return centred * lax.rsqrt(variance + 1e-05)


def one_hot(rows, index):
    places = lax.broadcasted_iota(jnp.int32, (rows, index.shape[1]), 0)
    return (places == index).astype(F32).astype(BF)


def shift_of(size):
    assert size & (size - 1) == 0
    return size.bit_length() - 1


def split(values):
    high = lax.shift_right_logical(values, shift_of(RADIX))
    return high.astype(F32), (values - high * RADIX).astype(F32)


def join(rows):
    return (rows[0:1] * RADIX + rows[1:2]).astype(jnp.int32)


def geometry_rows(weights, height):
    count, width = weights.shape
    return jnp.concatenate(
        [
            jnp.zeros((3, width), F32),
            0.5 * weights.astype(F32),
            jnp.zeros((height - 3 - count, width), F32),
        ],
        axis=0,
    )


def pack_kernel(
    sizes, count_ref, send_ref, recv_ref, feat_ref, msend_ref, mrecv_ref, mfeat_ref, pos_ref, cot_ref, out_ref, work_ref
):
    band, half, width, edges = sizes["band"], sizes["half"], sizes["width"], sizes["edges"]
    shard = sizes["shard"]
    b = lax.axis_index("mesh")
    live = count_ref[0] * BLOCK
    work_ref[...] = jnp.zeros_like(work_ref)
    senders = send_ref[...] - b * band
    high, low = split(senders)
    receivers = (recv_ref[...] - b * shard).astype(F32)
    features = feat_ref[...].astype(F32)
    alive = (lax.broadcasted_iota(jnp.int32, senders.shape, 1) < live).astype(F32)
    for part in range(2):
        lanes = slice(part * half, (part + 1) * half)
        base = part * 8
        work_ref[base : base + 1, 0:half] = high[:, lanes]
        work_ref[base + 1 : base + 2, 0:half] = low[:, lanes]
        work_ref[base + 2 : base + 3, 0:half] = receivers[:, lanes]
        work_ref[base + 3 : base + 7, 0:half] = features[:, lanes]
        work_ref[base + 7 : base + 8, 0:half] = alive[:, lanes]
    work_ref[:, half : half + width] = cot_ref[...].astype(F32)
    node = msend_ref[...]
    local = node - b * shard
    near = (local >= 0) & (local < shard)
    owner = lax.shift_right_logical(node, shift_of(PERIOD))
    far_band = lax.shift_right_logical(owner, shift_of(sizes["n_edge"]))
    step = lax.bitwise_xor(far_band, b)
    seat = lax.bitwise_and(owner, sizes["n_edge"] - 1)
    far = shard + ((step - 1) * sizes["n_edge"] + seat) * COARSE + lax.bitwise_and(node, PERIOD - 1)
    high, low = split(jnp.where(near, local, far))
    start = half + width
    work_ref[0:1, start : start + edges] = high
    work_ref[1:2, start : start + edges] = low
    work_ref[2:3, start : start + edges] = (mrecv_ref[...] - b * shard).astype(F32)
    work_ref[3:7, start : start + edges] = mfeat_ref[...].astype(F32)
    work_ref[8:11, start : start + sizes["rows"]] = pos_ref[...].astype(F32)
    out_ref[...] = work_ref[...].astype(BF)


def grid_kernel(grid_ref, first_ref, second_ref, inner_ref, geom_ref, table_ref, geom_out):
    hidden = silu(tn(grid_ref[...], first_ref[...])).astype(BF)
    latent = layer_norm(nn(hidden, second_ref[...])).astype(BF)
    table_ref[...] = (0.5 * nn(latent, inner_ref[...])).T.astype(BF)
    geom_out[...] = geometry_rows(geom_ref[...], 8).T.astype(BF)


def encode_kernel(sizes, chunk, *refs):
    n_edge, half, shard = sizes["n_edge"], sizes["half"], sizes["shard"]
    packs = refs[:n_edge]
    table_ref, geom_ref, out_ref, list_ref, acc_ref = refs[n_edge:]
    own = table_ref.shape[1]
    e = lax.axis_index("edge")
    per_half = half // chunk
    counts = []
    for d in range(n_edge):
        total = jnp.float32(0)
        for j in range(per_half):
            rows = packs[d][:, j * chunk : (j + 1) * chunk].astype(F32)
            list_ref[2 * per_half * d + j] = rows[0:8]
            list_ref[2 * per_half * d + per_half + j] = rows[8:16]
            total = total + jnp.sum(rows[7:8]) + jnp.sum(rows[15:16])
        counts.append((total.astype(jnp.int32) + (chunk - 1)) // chunk)
    acc_ref[...] = jnp.zeros_like(acc_ref)

    def body(step, carry):
        place = step
        before = jnp.int32(0)
        for d in range(n_edge):
            after = before + counts[d]
            inside = (step >= before) & (step < after)
            place = jnp.where(inside, 2 * per_half * d + step - before, place)
            before = after
        rows = list_ref[place]
        sender = join(rows) - e * own
        mine = (sender >= 0) & (sender < own) & (rows[7:8] > 0)
        receiver = jnp.where(mine, rows[2:3].astype(jnp.int32), -1)
        half_pre = nn(table_ref[...], one_hot(own, sender)) + nn(geom_ref[...], rows.astype(BF))
        act = (half_pre + half_pre * jnp.tanh(half_pre)).astype(BF)
        acc_ref[...] += nt(one_hot(shard, receiver), act)
        return carry

    lax.fori_loop(0, sum(counts), body, 0)
    out_ref[...] = acc_ref[...].astype(BF)


def node_kernel(sizes, parts_count, *refs):
    n_edge, rows, start = sizes["n_edge"], sizes["rows"], sizes["half"] + sizes["width"]
    packs, refs = refs[:n_edge], refs[n_edge:]
    parts, refs = refs[:parts_count], refs[parts_count:]
    outer_ref, first_ref, posw_ref, second_ref, latent_ref, coarse_ref, pos_ref, coarse_work = refs
    e = lax.axis_index("edge")
    posw = jnp.concatenate(
        [posw_ref[...].astype(F32), jnp.zeros((8 - posw_ref.shape[0], posw_ref.shape[1]), F32)], axis=0
    ).astype(BF)
    for d in range(n_edge):
        block = packs[d][:, start : start + 128].astype(F32)[8:16].T[0:rows].astype(BF)
        seat = pl.multiple_of(lax.bitwise_xor(e, d) * rows, rows)
        pos_ref[pl.ds(seat, rows), :] = nn(block, posw)
    total = parts[0][...].astype(F32)
    for part in parts[1:]:
        total = total + part[...].astype(F32)
    enc_sum = nn(total.astype(BF), outer_ref[...]).astype(BF)
    hidden = silu(nn(enc_sum, first_ref[...]) + pos_ref[...]).astype(BF)
    latent = layer_norm(nn(hidden, second_ref[...]))
    latent_ref[...] = latent.astype(BF)
    for d in range(n_edge):
        coarse_work[d * COARSE : (d + 1) * COARSE] = latent[d * rows : d * rows + COARSE]
    coarse_ref[...] = coarse_work[...].astype(BF)


def process_kernel(sizes, *refs):
    n_edge, n_mesh, rows, shard = sizes["n_edge"], sizes["n_mesh"], sizes["rows"], sizes["shard"]
    half, width, edges = sizes["half"], sizes["width"], sizes["edges"]
    packs, refs = refs[:n_edge], refs[n_edge:]
    latent_ref, refs = refs[0], refs[1:]
    coarse, refs = refs[: n_mesh - 1], refs[n_mesh - 1 :]
    send_w, recv_w, geom_w, outer_w, message_w, state_w, update_w = refs[:7]
    refs = refs[7:]
    far_out, refs = refs[: n_mesh - 1], refs[n_mesh - 1 :]
    keep_ref, cot_ref, slope_ref, stack_ref = refs
    e = lax.axis_index("edge")
    start = half + width
    lists = []
    for d in range(n_edge):
        lists.append(packs[d][:, start : start + edges])
        seat = pl.multiple_of(lax.bitwise_xor(e, d) * rows, rows)
        cot_ref[pl.ds(seat, rows), :] = packs[d][:, half : half + width]
    lists = jnp.concatenate(lists, axis=1)
    values = lists.astype(F32)[0:8]
    sender = join(values)
    receiver = values[2:3].astype(jnp.int32)
    latent = latent_ref[...]
    table = jnp.concatenate([latent] + [c[...] for c in coarse], axis=0)
    near_far = table.shape[0]
    products = jnp.concatenate(
        [
            (0.5 * nn(table, send_w[...])).astype(BF),
            (0.5 * nn(latent, recv_w[...])).astype(BF),
            geometry_rows(geom_w[...], 16).astype(BF),
        ],
        axis=0,
    )
    pick_receiver = one_hot(shard, receiver)
    picks = jnp.concatenate([one_hot(near_far, sender), pick_receiver, lists], axis=0)
    half_pre = tn(products, picks)
    bend = jnp.tanh(half_pre)
    act = (half_pre + half_pre * bend).astype(BF)
    slope_ref[...] = 0.5 * (1.0 + bend) * (1.0 + half_pre * (1.0 - bend))
    proc_sum = nn(nt(pick_receiver, act).astype(BF), outer_w[...]).astype(BF)
    update_pre = nn(proc_sum, message_w[...]) + nn(latent, state_w[...])
    update_act = silu(update_pre).astype(BF)
    grad_pre = (nt(cot_ref[...], update_w[...]) * silu_grad(update_pre)).astype(BF)
    grad_sum = nt(grad_pre, message_w[...]).astype(BF)
    grad_act = nt(grad_sum, outer_w[...]).astype(BF)
    grad_edge = (tn(grad_act, pick_receiver) * slope_ref[...]).astype(BF)
    far = sender - shard
    far_seat = lax.bitwise_and(lax.shift_right_logical(far, shift_of(COARSE)), n_edge - 1)
    far_row = lax.shift_right_logical(far, shift_of(COARSE * n_edge)) * COARSE + lax.bitwise_and(far, COARSE - 1)
    far_row = jnp.where((far >= 0) & (far_seat == e), far_row, -1)
    far_height = -(-(n_mesh - 1) * COARSE // 16) * 16
    near_row = jnp.where(far < 0, sender - e * rows, -1)
    spread = jnp.concatenate(
        [one_hot(far_height, far_row), one_hot(rows, near_row), one_hot(rows, receiver - e * rows)], axis=0
    )
    sums = nt(spread, grad_edge).astype(BF)
    returned = nt(sums[0:far_height], send_w[...])
    for m in range(n_mesh - 1):
        far_out[m][...] = returned[m * COARSE : (m + 1) * COARSE]
    stack_ref[0] = latent
    stack_ref[1] = update_act
    stack_ref[2] = grad_pre
    stack_ref[3] = cot_ref[...]
    seat = pl.multiple_of(e * rows, rows)
    for k in range(4):
        keep_ref[k] = stack_ref[k, pl.ds(seat, rows), :]
    keep_ref[4] = sums[far_height : far_height + rows]
    keep_ref[5] = sums[far_height + rows : far_height + 2 * rows]


def finish_kernel(keep_ref, send_w, recv_w, state_w, update_w, out_ref, base_ref):
    out_ref[...] = (keep_ref[0].astype(F32) + nn(keep_ref[1], update_w[...])).astype(BF)
    base_ref[...] = (
        keep_ref[3].astype(F32)
        + nt(keep_ref[2], state_w[...])
        + nt(keep_ref[4], send_w[...])
        + nt(keep_ref[5], recv_w[...])
    )


def close_kernel(base_ref, *refs):
    returned, out_ref = refs[:-1], refs[-1]
    total = returned[0][...]
    for part in returned[1:]:
        total = total + part[...]
    out_ref[...] = base_ref[...]
    out_ref[0:COARSE] = base_ref[0:COARSE] + total


def call(kernel, name, outs, scratch=(), specs=None, limit=16 << 20):
    def run(*args):
        return pl.pallas_call(
            kernel,
            name=name,
            out_shape=[jax.ShapeDtypeStruct(shape, dtype) for shape, dtype in outs],
            in_specs=specs or [IN_VMEM] * len(args),
            out_specs=[IN_VMEM] * len(outs),
            scratch_shapes=list(scratch),
            compiler_params=pltpu.CompilerParams(vmem_limit_bytes=limit),
        )(*args)

    return run


def partner(value, axis, size, step):
    return lax.ppermute(value, axis, [(i, i ^ step) for i in range(size)])


def shards(
    grid_input,
    mesh_position,
    encoder_senders,
    encoder_receivers,
    encoder_features,
    encoder_counts,
    mesh_senders,
    mesh_receivers,
    mesh_features,
    cotangent,
    grid_first,
    grid_second,
    encoder_inner,
    encoder_geometry,
    encoder_outer,
    node_first,
    node_position,
    node_second,
    edge_sender,
    edge_receiver,
    edge_geometry,
    edge_outer,
    update_message,
    update_state,
    update_outer,
):
    n_edge, n_mesh = lax.axis_size("edge"), lax.axis_size("mesh")
    own, width = grid_input.shape[0], grid_second.shape[1]
    rows, slots, edges = mesh_position.shape[1], encoder_senders.shape[0], mesh_senders.shape[0]
    shard, half = rows * n_edge, encoder_senders.shape[0] // 2
    assert rows == PERIOD and n_edge & (n_edge - 1) == 0 and n_mesh & (n_mesh - 1) == 0
    sizes = dict(
        n_edge=n_edge, n_mesh=n_mesh, rows=rows, shard=shard, half=half, width=width, edges=edges, band=own * n_edge
    )
    lanes = half + width + edges
    (pack,) = call(
        functools.partial(pack_kernel, sizes),
        "pack",
        [((16, lanes), BF)],
        [pltpu.VMEM((16, lanes), F32)],
        [IN_SMEM] + [IN_VMEM] * 8,
    )(
        encoder_counts,
        encoder_senders.reshape(1, slots),
        encoder_receivers.reshape(1, slots),
        encoder_features,
        mesh_senders.reshape(1, edges),
        mesh_receivers.reshape(1, edges),
        mesh_features,
        mesh_position,
        cotangent,
    )
    packs = [pack] + [partner(pack, "edge", n_edge, m) for m in range(1, n_edge)]
    table, geometry = call(grid_kernel, "grid", [((width, own), BF), ((width, 8), BF)])(
        grid_input.T, grid_first, grid_second, encoder_inner, encoder_geometry
    )
    chunk = min(512, half)
    (partial,) = call(
        functools.partial(encode_kernel, sizes, chunk),
        "encode",
        [((shard, width), BF)],
        [pltpu.VMEM((n_edge * slots // chunk, 8, chunk), F32), pltpu.VMEM((shard, width), F32)],
    )(*packs, table, geometry)
    parts = [partial] + [partner(partial, "edge", n_edge, m) for m in range(1, n_edge)]
    latent, coarse = call(
        functools.partial(node_kernel, sizes, len(parts)),
        "node",
        [((shard, width), BF), ((n_edge * COARSE, width), BF)],
        [pltpu.VMEM((shard, width), F32), pltpu.VMEM((n_edge * COARSE, width), F32)],
    )(*packs, *parts, encoder_outer, node_first, node_position, node_second)
    others = [partner(coarse, "mesh", n_mesh, m) for m in range(1, n_mesh)]
    *far, keep = call(
        functools.partial(process_kernel, sizes),
        "process",
        [((COARSE, width), F32)] * (n_mesh - 1) + [((6, rows, width), BF)],
        [
            pltpu.VMEM((shard, width), BF),
            pltpu.VMEM((width, edges * n_edge), F32),
            pltpu.VMEM((4, shard, width), BF),
        ],
    )(
        *packs,
        latent,
        *others,
        edge_sender,
        edge_receiver,
        edge_geometry,
        edge_outer,
        update_message,
        update_state,
        update_outer,
    )
    returned = [partner(far[m - 1], "mesh", n_mesh, m) for m in range(1, n_mesh)]
    output, base = call(finish_kernel, "finish", [((rows, width), BF), ((rows, width), F32)])(
        keep, edge_sender, edge_receiver, update_state, update_outer
    )
    (gradient,) = call(close_kernel, "close", [((rows, width), F32)])(base, *returned)
    return (output, gradient)


def solution(mesh):
    nodes = P(("groups", "mesh", "edge"), None)
    flat = P(("mesh", "edge"))
    lanes = P(None, ("mesh", "edge"))
    in_specs = (nodes, lanes, flat, flat, lanes, flat, flat, flat, lanes, nodes) + (P(),) * 15
    return jax.shard_map(shards, mesh=mesh, in_specs=in_specs, out_specs=(nodes, nodes), check_vma=False)
```

```python
import functools

import jax
import jax.numpy as jnp
from jax import lax
from jax.experimental import pallas as pl
from jax.experimental.pallas import tpu as pltpu
from jax.sharding import PartitionSpec as P

BLOCK = 128
PERIOD = 16
COARSE = 4
RADIX = 256
BF = jnp.bfloat16
F32 = jnp.float32
IN_VMEM = pl.BlockSpec(memory_space=pltpu.VMEM)
IN_SMEM = pl.BlockSpec(memory_space=pltpu.SMEM)
IN_HBM = pl.BlockSpec(memory_space=pltpu.HBM)


def nn(left, right):
    return jnp.dot(left, right, preferred_element_type=F32)


def nt(left, right):
    return lax.dot_general(left, right, (((1,), (1,)), ((), ())), preferred_element_type=F32)


def tn(left, right):
    return lax.dot_general(left, right, (((0,), (0,)), ((), ())), preferred_element_type=F32)


def silu(values):
    half = 0.5 * values
    return half + half * jnp.tanh(half)


def silu_grad(values):
    half = 0.5 * values
    bend = jnp.tanh(half)
    return 0.5 * (1.0 + bend) * (1.0 + half * (1.0 - bend))


def layer_norm(values):
    centred = values - jnp.mean(values, axis=-1, keepdims=True)
    variance = jnp.mean(centred * centred, axis=-1, keepdims=True)
    return centred * lax.rsqrt(variance + 1e-05)


def one_hot(rows, index):
    places = lax.broadcasted_iota(jnp.int32, (rows, index.shape[1]), 0)
    return (places == index).astype(F32).astype(BF)


def shift_of(size):
    assert size & (size - 1) == 0
    return size.bit_length() - 1


def split(values):
    high = lax.shift_right_logical(values, shift_of(RADIX))
    return high.astype(F32), (values - high * RADIX).astype(F32)


def join(rows):
    return (rows[0:1] * RADIX + rows[1:2]).astype(jnp.int32)


def geometry_rows(weights, height):
    count, width = weights.shape
    return jnp.concatenate(
        [
            jnp.zeros((3, width), F32),
            0.5 * weights.astype(F32),
            jnp.zeros((height - 3 - count, width), F32),
        ],
        axis=0,
    )


def fetch(sources, targets, sems):
    copies = [pltpu.make_async_copy(s, t, sems.at[k]) for k, (s, t) in enumerate(zip(sources, targets))]
    for copy in copies:
        copy.start()
    return copies


def pack_kernel(sizes, count_ref, *refs):
    sources, out_ref, work_ref, targets, sems = refs[:8], refs[8], refs[9], refs[10:18], refs[18]
    for copy in fetch(sources, targets, sems):
        copy.wait()
    send_ref, recv_ref, feat_ref, msend_ref, mrecv_ref, mfeat_ref, pos_ref, cot_ref = targets
    band, half, width, edges = sizes["band"], sizes["half"], sizes["width"], sizes["edges"]
    shard = sizes["shard"]
    b = lax.axis_index("mesh")
    live = count_ref[0] * BLOCK
    work_ref[...] = jnp.zeros_like(work_ref)
    senders = send_ref[...] - b * band
    high, low = split(senders)
    receivers = (recv_ref[...] - b * shard).astype(F32)
    features = feat_ref[...].astype(F32)
    alive = (lax.broadcasted_iota(jnp.int32, senders.shape, 1) < live).astype(F32)
    for part in range(2):
        lanes = slice(part * half, (part + 1) * half)
        base = part * 8
        work_ref[base : base + 1, 0:half] = high[:, lanes]
        work_ref[base + 1 : base + 2, 0:half] = low[:, lanes]
        work_ref[base + 2 : base + 3, 0:half] = receivers[:, lanes]
        work_ref[base + 3 : base + 7, 0:half] = features[:, lanes]
        work_ref[base + 7 : base + 8, 0:half] = alive[:, lanes]
    work_ref[:, half : half + width] = cot_ref[...].astype(F32)
    node = msend_ref[...]
    local = node - b * shard
    near = (local >= 0) & (local < shard)
    owner = lax.shift_right_logical(node, shift_of(PERIOD))
    far_band = lax.shift_right_logical(owner, shift_of(sizes["n_edge"]))
    step = lax.bitwise_xor(far_band, b)
    seat = lax.bitwise_and(owner, sizes["n_edge"] - 1)
    far = shard + ((step - 1) * sizes["n_edge"] + seat) * COARSE + lax.bitwise_and(node, PERIOD - 1)
    high, low = split(jnp.where(near, local, far))
    start = half + width
    work_ref[0:1, start : start + edges] = high
    work_ref[1:2, start : start + edges] = low
    work_ref[2:3, start : start + edges] = (mrecv_ref[...] - b * shard).astype(F32)
    work_ref[3:7, start : start + edges] = mfeat_ref[...].astype(F32)
    work_ref[8:11, start : start + sizes["rows"]] = pos_ref[...].astype(F32)
    out_ref[...] = work_ref[...].astype(BF)


def grid_kernel(geom_ref, *refs):
    sources, table_ref, geom_out, targets, sems = refs[:4], refs[4], refs[5], refs[6:10], refs[10]
    copies = fetch(sources, targets, sems)
    grid_ref, first_ref, second_ref, inner_ref = targets
    copies[0].wait()
    copies[1].wait()
    hidden = silu(tn(grid_ref[...], first_ref[...])).astype(BF)
    copies[2].wait()
    latent = layer_norm(nn(hidden, second_ref[...])).astype(BF)
    copies[3].wait()
    table_ref[...] = (0.5 * nn(latent, inner_ref[...])).T.astype(BF)
    geom_out[...] = geometry_rows(geom_ref[...], 8).T.astype(BF)


def encode_kernel(sizes, chunk, *refs):
    n_edge, half, shard = sizes["n_edge"], sizes["half"], sizes["shard"]
    packs = refs[:n_edge]
    table_ref, geom_ref, out_ref, list_ref, acc_ref = refs[n_edge:]
    own = table_ref.shape[1]
    e = lax.axis_index("edge")
    per_half = half // BLOCK
    blocks = jnp.int32(0)
    for d in range(n_edge):
        pack = packs[d][:, 0:half].astype(F32)
        for j in range(per_half):
            rows = pack[:, j * BLOCK : (j + 1) * BLOCK]
            list_ref[blocks + j] = rows[0:8]
            list_ref[blocks + per_half + j] = rows[8:16]
        total = jnp.sum(pack[7:8] + pack[15:16]).astype(jnp.int32)
        blocks = blocks + lax.shift_right_logical(total, shift_of(BLOCK))
    group = chunk // BLOCK
    for j in range(group):
        list_ref[blocks + j] = jnp.zeros((8, BLOCK), F32)
    acc_ref[...] = jnp.zeros_like(acc_ref)

    def body(step, carry):
        rows = jnp.concatenate([list_ref[step * group + j] for j in range(group)], axis=1)
        sender = join(rows) - e * own
        mine = (sender >= 0) & (sender < own) & (rows[7:8] > 0)
        receiver = jnp.where(mine, rows[2:3].astype(jnp.int32), -1)
        half_pre = nn(table_ref[...], one_hot(own, sender)) + nn(geom_ref[...], rows.astype(BF))
        act = (half_pre + half_pre * jnp.tanh(half_pre)).astype(BF)
        acc_ref[...] += nt(one_hot(shard, receiver), act)
        return carry

    lax.fori_loop(0, (blocks + (group - 1)) // group, body, 0)
    out_ref[...] = acc_ref[...].astype(BF)


def node_kernel(sizes, parts_count, *refs):
    n_edge, rows, start = sizes["n_edge"], sizes["rows"], sizes["half"] + sizes["width"]
    packs, refs = refs[:n_edge], refs[n_edge:]
    parts, refs = refs[:parts_count], refs[parts_count:]
    outer_ref, first_ref, posw_ref, second_ref, latent_ref, coarse_ref, pos_ref, coarse_work = refs
    e = lax.axis_index("edge")
    posw = jnp.concatenate(
        [posw_ref[...].astype(F32), jnp.zeros((8 - posw_ref.shape[0], posw_ref.shape[1]), F32)], axis=0
    ).astype(BF)
    for d in range(n_edge):
        block = packs[d][:, start : start + 128].astype(F32)[8:16].T[0:rows].astype(BF)
        seat = pl.multiple_of(lax.bitwise_xor(e, d) * rows, rows)
        pos_ref[pl.ds(seat, rows), :] = nn(block, posw)
    total = parts[0][...].astype(F32)
    for part in parts[1:]:
        total = total + part[...].astype(F32)
    enc_sum = nn(total.astype(BF), outer_ref[...]).astype(BF)
    hidden = silu(nn(enc_sum, first_ref[...]) + pos_ref[...]).astype(BF)
    latent = layer_norm(nn(hidden, second_ref[...]))
    latent_ref[...] = latent.astype(BF)
    for d in range(n_edge):
        coarse_work[d * COARSE : (d + 1) * COARSE] = latent[d * rows : d * rows + COARSE]
    coarse_ref[...] = coarse_work[...].astype(BF)


def process_kernel(sizes, *refs):
    n_edge, n_mesh, rows, shard = sizes["n_edge"], sizes["n_mesh"], sizes["rows"], sizes["shard"]
    half, width, edges = sizes["half"], sizes["width"], sizes["edges"]
    packs, refs = refs[:n_edge], refs[n_edge:]
    latent_ref, refs = refs[0], refs[1:]
    coarse, refs = refs[: n_mesh - 1], refs[n_mesh - 1 :]
    send_w, recv_w, geom_w, outer_w, message_w, state_w, update_w = refs[:7]
    refs = refs[7:]
    far_out, refs = refs[: n_mesh - 1], refs[n_mesh - 1 :]
    keep_ref, cot_ref, slope_ref, stack_ref = refs
    e = lax.axis_index("edge")
    start = half + width
    lists = []
    for d in range(n_edge):
        lists.append(packs[d][:, start : start + edges])
        seat = pl.multiple_of(lax.bitwise_xor(e, d) * rows, rows)
        cot_ref[pl.ds(seat, rows), :] = packs[d][:, half : half + width]
    lists = jnp.concatenate(lists, axis=1)
    values = lists.astype(F32)[0:8]
    sender = join(values)
    receiver = values[2:3].astype(jnp.int32)
    latent = latent_ref[...]
    table = jnp.concatenate([latent] + [c[...] for c in coarse], axis=0)
    near_far = table.shape[0]
    products = jnp.concatenate(
        [
            (0.5 * nn(table, send_w[...])).astype(BF),
            (0.5 * nn(latent, recv_w[...])).astype(BF),
            geometry_rows(geom_w[...], 16).astype(BF),
        ],
        axis=0,
    )
    pick_receiver = one_hot(shard, receiver)
    picks = jnp.concatenate([one_hot(near_far, sender), pick_receiver, lists], axis=0)
    half_pre = tn(products, picks)
    bend = jnp.tanh(half_pre)
    act = (half_pre + half_pre * bend).astype(BF)
    slope_ref[...] = 0.5 * (1.0 + bend) * (1.0 + half_pre * (1.0 - bend))
    proc_sum = nn(nt(pick_receiver, act).astype(BF), outer_w[...]).astype(BF)
    update_pre = nn(proc_sum, message_w[...]) + nn(latent, state_w[...])
    update_act = silu(update_pre).astype(BF)
    grad_pre = (nt(cot_ref[...], update_w[...]) * silu_grad(update_pre)).astype(BF)
    grad_sum = nt(grad_pre, message_w[...]).astype(BF)
    grad_act = nt(grad_sum, outer_w[...]).astype(BF)
    grad_edge = (tn(grad_act, pick_receiver) * slope_ref[...]).astype(BF)
    far = sender - shard
    far_seat = lax.bitwise_and(lax.shift_right_logical(far, shift_of(COARSE)), n_edge - 1)
    far_row = lax.shift_right_logical(far, shift_of(COARSE * n_edge)) * COARSE + lax.bitwise_and(far, COARSE - 1)
    far_row = jnp.where((far >= 0) & (far_seat == e), far_row, -1)
    far_height = -(-(n_mesh - 1) * COARSE // 16) * 16
    near_row = jnp.where(far < 0, sender - e * rows, -1)
    spread = jnp.concatenate(
        [one_hot(far_height, far_row), one_hot(rows, near_row), one_hot(rows, receiver - e * rows)], axis=0
    )
    sums = nt(spread, grad_edge).astype(BF)
    returned = nt(sums[0:far_height], send_w[...])
    for m in range(n_mesh - 1):
        far_out[m][...] = returned[m * COARSE : (m + 1) * COARSE]
    stack_ref[0] = latent
    stack_ref[1] = update_act
    stack_ref[2] = grad_pre
    stack_ref[3] = cot_ref[...]
    seat = pl.multiple_of(e * rows, rows)
    for k in range(4):
        keep_ref[k] = stack_ref[k, pl.ds(seat, rows), :]
    keep_ref[4] = sums[far_height : far_height + rows]
    keep_ref[5] = sums[far_height + rows : far_height + 2 * rows]


def finish_kernel(keep_ref, send_w, recv_w, state_w, update_w, out_ref, base_ref):
    out_ref[...] = (keep_ref[0].astype(F32) + nn(keep_ref[1], update_w[...])).astype(BF)
    base_ref[...] = (
        keep_ref[3].astype(F32)
        + nt(keep_ref[2], state_w[...])
        + nt(keep_ref[4], send_w[...])
        + nt(keep_ref[5], recv_w[...])
    )


def close_kernel(base_ref, *refs):
    returned, out_ref = refs[:-1], refs[-1]
    total = returned[0][...]
    for part in returned[1:]:
        total = total + part[...]
    out_ref[...] = base_ref[...]
    out_ref[0:COARSE] = base_ref[0:COARSE] + total


def call(kernel, name, outs, scratch=(), specs=None, limit=16 << 20):
    def run(*args):
        return pl.pallas_call(
            kernel,
            name=name,
            out_shape=[jax.ShapeDtypeStruct(shape, dtype) for shape, dtype in outs],
            in_specs=specs or [IN_VMEM] * len(args),
            out_specs=[IN_VMEM] * len(outs),
            scratch_shapes=list(scratch),
            compiler_params=pltpu.CompilerParams(vmem_limit_bytes=limit),
        )(*args)

    return run


def in_hbm(value):
    return pltpu.with_memory_space_constraint(value, pltpu.HBM)


def partner(value, axis, size, step):
    return lax.ppermute(value, axis, [(i, i ^ step) for i in range(size)])


def shards(
    grid_input,
    mesh_position,
    encoder_senders,
    encoder_receivers,
    encoder_features,
    encoder_counts,
    mesh_senders,
    mesh_receivers,
    mesh_features,
    cotangent,
    grid_first,
    grid_second,
    encoder_inner,
    encoder_geometry,
    encoder_outer,
    node_first,
    node_position,
    node_second,
    edge_sender,
    edge_receiver,
    edge_geometry,
    edge_outer,
    update_message,
    update_state,
    update_outer,
):
    n_edge, n_mesh = lax.axis_size("edge"), lax.axis_size("mesh")
    own, width = grid_input.shape[0], grid_second.shape[1]
    rows, slots, edges = mesh_position.shape[1], encoder_senders.shape[0], mesh_senders.shape[0]
    shard, half = rows * n_edge, encoder_senders.shape[0] // 2
    assert rows == PERIOD and n_edge & (n_edge - 1) == 0 and n_mesh & (n_mesh - 1) == 0
    sizes = dict(
        n_edge=n_edge, n_mesh=n_mesh, rows=rows, shard=shard, half=half, width=width, edges=edges, band=own * n_edge
    )
    lanes = half + width + edges
    lists = (
        encoder_senders.reshape(1, slots),
        encoder_receivers.reshape(1, slots),
        encoder_features,
        mesh_senders.reshape(1, edges),
        mesh_receivers.reshape(1, edges),
        mesh_features,
        mesh_position,
        cotangent,
    )
    (pack,) = call(
        functools.partial(pack_kernel, sizes),
        "pack",
        [((16, lanes), BF)],
        [pltpu.VMEM((16, lanes), F32)] + [pltpu.VMEM(v.shape, v.dtype) for v in lists] + [pltpu.SemaphoreType.DMA((8,))],
        [IN_SMEM] + [IN_HBM] * 8,
    )(encoder_counts, *[in_hbm(v) for v in lists])
    packs = [pack] + [partner(pack, "edge", n_edge, m) for m in range(1, n_edge)]
    grid_operands = (grid_input.T, grid_first, grid_second, encoder_inner)
    table, geometry = call(
        grid_kernel,
        "grid",
        [((width, own), BF), ((width, 8), BF)],
        [pltpu.VMEM(v.shape, v.dtype) for v in grid_operands] + [pltpu.SemaphoreType.DMA((4,))],
        [IN_VMEM] + [IN_HBM] * 4,
    )(encoder_geometry, *[in_hbm(v) for v in grid_operands])
    chunk = min(512, half)
    (partial,) = call(
        functools.partial(encode_kernel, sizes, chunk),
        "encode",
        [((shard, width), BF)],
        [pltpu.VMEM((n_edge * slots // BLOCK + chunk // BLOCK, 8, BLOCK), F32), pltpu.VMEM((shard, width), F32)],
    )(*packs, table, geometry)
    parts = [partial] + [partner(partial, "edge", n_edge, m) for m in range(1, n_edge)]
    latent, coarse = call(
        functools.partial(node_kernel, sizes, len(parts)),
        "node",
        [((shard, width), BF), ((n_edge * COARSE, width), BF)],
        [pltpu.VMEM((shard, width), F32), pltpu.VMEM((n_edge * COARSE, width), F32)],
    )(*packs, *parts, encoder_outer, node_first, node_position, node_second)
    others = [partner(coarse, "mesh", n_mesh, m) for m in range(1, n_mesh)]
    *far, keep = call(
        functools.partial(process_kernel, sizes),
        "process",
        [((COARSE, width), F32)] * (n_mesh - 1) + [((6, rows, width), BF)],
        [
            pltpu.VMEM((shard, width), BF),
            pltpu.VMEM((width, edges * n_edge), F32),
            pltpu.VMEM((4, shard, width), BF),
        ],
    )(
        *packs,
        latent,
        *others,
        edge_sender,
        edge_receiver,
        edge_geometry,
        edge_outer,
        update_message,
        update_state,
        update_outer,
    )
    returned = [partner(far[m - 1], "mesh", n_mesh, m) for m in range(1, n_mesh)]
    output, base = call(finish_kernel, "finish", [((rows, width), BF), ((rows, width), F32)])(
        keep, edge_sender, edge_receiver, update_state, update_outer
    )
    (gradient,) = call(close_kernel, "close", [((rows, width), F32)])(base, *returned)
    return (output, gradient)


def solution(mesh):
    nodes = P(("groups", "mesh", "edge"), None)
    flat = P(("mesh", "edge"))
    lanes = P(None, ("mesh", "edge"))
    in_specs = (nodes, lanes, flat, flat, lanes, flat, flat, flat, lanes, nodes) + (P(),) * 15
    return jax.shard_map(shards, mesh=mesh, in_specs=in_specs, out_specs=(nodes, nodes), check_vma=False)
```

```python
import functools

import jax
import jax.numpy as jnp
from jax import lax
from jax.experimental import pallas as pl
from jax.experimental.pallas import tpu as pltpu
from jax.sharding import PartitionSpec as P

BLOCK = 128
PERIOD = 16
COARSE = 4
RADIX = 256
BF = jnp.bfloat16
F32 = jnp.float32
IN_VMEM = pl.BlockSpec(memory_space=pltpu.VMEM)
IN_SMEM = pl.BlockSpec(memory_space=pltpu.SMEM)
IN_HBM = pl.BlockSpec(memory_space=pltpu.HBM)


def nn(left, right):
    return jnp.dot(left, right, preferred_element_type=F32)


def nt(left, right):
    return lax.dot_general(left, right, (((1,), (1,)), ((), ())), preferred_element_type=F32)


def tn(left, right):
    return lax.dot_general(left, right, (((0,), (0,)), ((), ())), preferred_element_type=F32)


def silu(values):
    half = 0.5 * values
    return half + half * jnp.tanh(half)


def silu_grad(values):
    half = 0.5 * values
    bend = jnp.tanh(half)
    return 0.5 * (1.0 + bend) * (1.0 + half * (1.0 - bend))


def layer_norm(values):
    centred = values - jnp.mean(values, axis=-1, keepdims=True)
    variance = jnp.mean(centred * centred, axis=-1, keepdims=True)
    return centred * lax.rsqrt(variance + 1e-05)


def one_hot(rows, index):
    places = lax.broadcasted_iota(jnp.int32, (rows, index.shape[1]), 0)
    return (places == index).astype(F32).astype(BF)


def shift_of(size):
    assert size & (size - 1) == 0
    return size.bit_length() - 1


def split(values):
    high = lax.shift_right_logical(values, shift_of(RADIX))
    return high.astype(F32), (values - high * RADIX).astype(F32)


def join(rows):
    return (rows[0:1] * RADIX + rows[1:2]).astype(jnp.int32)


def geometry_rows(weights, height):
    count, width = weights.shape
    return jnp.concatenate(
        [
            jnp.zeros((3, width), F32),
            0.5 * weights.astype(F32),
            jnp.zeros((height - 3 - count, width), F32),
        ],
        axis=0,
    )


def fetch(sources, targets, sems):
    copies = [pltpu.make_async_copy(s, t, sems.at[k]) for k, (s, t) in enumerate(zip(sources, targets))]
    for copy in copies:
        copy.start()
    return copies


def pack_kernel(sizes, count_ref, *refs):
    sources, out_ref, work_ref, targets, sems = refs[:8], refs[8], refs[9], refs[10:18], refs[18]
    for copy in fetch(sources, targets, sems):
        copy.wait()
    send_ref, recv_ref, feat_ref, msend_ref, mrecv_ref, mfeat_ref, pos_ref, cot_ref = targets
    band, half, width, edges = sizes["band"], sizes["half"], sizes["width"], sizes["edges"]
    shard = sizes["shard"]
    b = lax.axis_index("mesh")
    live = count_ref[0] * BLOCK
    work_ref[...] = jnp.zeros_like(work_ref)
    senders = send_ref[...] - b * band
    high, low = split(senders)
    receivers = (recv_ref[...] - b * shard).astype(F32)
    features = feat_ref[...].astype(F32)
    alive = (lax.broadcasted_iota(jnp.int32, senders.shape, 1) < live).astype(F32)
    for part in range(2):
        lanes = slice(part * half, (part + 1) * half)
        base = part * 8
        work_ref[base : base + 1, 0:half] = high[:, lanes]
        work_ref[base + 1 : base + 2, 0:half] = low[:, lanes]
        work_ref[base + 2 : base + 3, 0:half] = receivers[:, lanes]
        work_ref[base + 3 : base + 7, 0:half] = features[:, lanes]
        work_ref[base + 7 : base + 8, 0:half] = alive[:, lanes]
    work_ref[:, half : half + width] = cot_ref[...].astype(F32)
    node = msend_ref[...]
    local = node - b * shard
    near = (local >= 0) & (local < shard)
    owner = lax.shift_right_logical(node, shift_of(PERIOD))
    far_band = lax.shift_right_logical(owner, shift_of(sizes["n_edge"]))
    step = lax.bitwise_xor(far_band, b)
    seat = lax.bitwise_and(owner, sizes["n_edge"] - 1)
    far = shard + ((step - 1) * sizes["n_edge"] + seat) * COARSE + lax.bitwise_and(node, PERIOD - 1)
    high, low = split(jnp.where(near, local, far))
    start = half + width
    work_ref[0:1, start : start + edges] = high
    work_ref[1:2, start : start + edges] = low
    work_ref[2:3, start : start + edges] = (mrecv_ref[...] - b * shard).astype(F32)
    work_ref[3:7, start : start + edges] = mfeat_ref[...].astype(F32)
    work_ref[8:11, start : start + sizes["rows"]] = pos_ref[...].astype(F32)
    out_ref[...] = work_ref[...].astype(BF)


def grid_kernel(geom_ref, *refs):
    sources, table_ref, geom_out, targets, sems = refs[:4], refs[4], refs[5], refs[6:10], refs[10]
    copies = fetch(sources, targets, sems)
    grid_ref, first_ref, second_ref, inner_ref = targets
    copies[0].wait()
    copies[1].wait()
    hidden = silu(tn(grid_ref[...], first_ref[...])).astype(BF)
    copies[2].wait()
    latent = layer_norm(nn(hidden, second_ref[...])).astype(BF)
    copies[3].wait()
    table_ref[...] = (0.5 * nn(latent, inner_ref[...])).T.astype(BF)
    geom_out[...] = geometry_rows(geom_ref[...], 8).T.astype(BF)


SORT = 6
SLOTS = 256
PAIR = 2


def encode_kernel(sizes, *refs):
    n_edge, half, shard = sizes["n_edge"], sizes["half"], sizes["shard"]
    packs = refs[:n_edge]
    table_ref, geom_ref, out_ref, list_ref, mine_ref, rank_ref, acc_ref = refs[n_edge:]
    own, height = table_ref.shape[1], mine_ref.shape[0]
    e = lax.axis_index("edge")
    per_half = half // BLOCK
    mine_ref[...] = jnp.zeros_like(mine_ref)
    blocks = jnp.int32(0)
    for d in range(n_edge):
        pack = packs[d][:, 0:half].astype(F32)
        for part in range(2):
            rows = pack[8 * part : 8 * part + 8]
            sender = join(rows) - e * own
            mine = ((sender >= 0) & (sender < own) & (rows[7:8] > 0)).astype(F32)
            for j in range(per_half):
                lanes = slice(j * BLOCK, (j + 1) * BLOCK)
                list_ref[blocks + part * per_half + j] = rows[:, lanes]
                mine_ref[pl.ds(blocks + part * per_half + j, 1), :] = mine[:, lanes]
        total = jnp.sum(pack[7:8] + pack[15:16]).astype(jnp.int32)
        blocks = blocks + lax.shift_right_logical(total, shift_of(BLOCK))
    for j in range(SORT * PAIR):
        list_ref[blocks + j] = jnp.zeros((8, BLOCK), F32)
    mine = mine_ref[...]
    first = lax.broadcasted_iota(jnp.int32, (BLOCK, 2 * BLOCK), 0)
    second = lax.broadcasted_iota(jnp.int32, (BLOCK, 2 * BLOCK), 1)
    within = nn(mine.astype(BF), (first <= second).astype(F32).astype(BF))
    first = lax.broadcasted_iota(jnp.int32, (height, height), 0)
    second = lax.broadcasted_iota(jnp.int32, (height, height), 1)
    inverse = (1 << 16) // SORT + 1
    same = lax.shift_right_logical(first * inverse, 16) == lax.shift_right_logical(second * inverse, 16)
    before = nn(((second < first) & same).astype(F32).astype(BF), within[:, BLOCK:].astype(BF))
    rank = jnp.where(mine > 0, within[:, :BLOCK] + before - 1.0, -1.0)
    rank_ref[...] = rank.astype(jnp.int32)
    rounds = lax.shift_right_logical(jnp.max(rank).astype(jnp.int32) + SLOTS, shift_of(SLOTS))
    acc_ref[...] = jnp.zeros_like(acc_ref)

    def body(step, base):
        drawn = []
        for k in range(PAIR):
            seats = [(step * PAIR + k) * SORT + j for j in range(SORT)]
            rows = jnp.concatenate([list_ref[seat] for seat in seats], axis=1)
            picks = [one_hot(SLOTS, rank_ref[pl.ds(seat, 1), :] - base) for seat in seats]
            drawn.append(nt(rows.astype(BF), jnp.concatenate(picks, axis=1)))
        rows = jnp.concatenate(drawn, axis=1)
        sender = join(rows) - e * own
        receiver = jnp.where(rows[7:8] > 0, rows[2:3].astype(jnp.int32), -1)
        half_pre = nn(table_ref[...], one_hot(own, sender)) + nn(geom_ref[...], rows.astype(BF))
        act = (half_pre + half_pre * jnp.tanh(half_pre)).astype(BF)
        acc_ref[...] += nt(one_hot(shard, receiver), act)
        return base

    steps = lax.div(blocks + (SORT * PAIR - 1), SORT * PAIR)

    def sweep(turn, carry):
        lax.fori_loop(0, steps, body, turn * SLOTS)
        return carry

    lax.fori_loop(0, rounds, sweep, 0)
    out_ref[...] = acc_ref[...].astype(BF)


def prep_kernel(sizes, *refs):
    n_edge, n_mesh, rows, shard = sizes["n_edge"], sizes["n_mesh"], sizes["rows"], sizes["shard"]
    half, width, edges = sizes["half"], sizes["width"], sizes["edges"]
    packs, refs = refs[:n_edge], refs[n_edge:]
    posw_ref, enc_ref, first_ref, outer_ref, message_ref, update_ref = refs[1:7]
    enter_ref, pass_ref, pos_ref, slope_ref, picks_ref, spread_ref, own_ref, cot_ref = refs[7:]
    e = lax.axis_index("edge")
    start = half + width
    enter_ref[...] = nn(enc_ref[...], first_ref[...]).astype(BF)
    pass_ref[...] = nn(outer_ref[...], message_ref[...]).astype(BF)
    posw = jnp.concatenate(
        [posw_ref[...].astype(F32), jnp.zeros((8 - posw_ref.shape[0], width), F32)], axis=0
    ).astype(BF)
    for d in range(n_edge):
        seat = pl.multiple_of(lax.bitwise_xor(e, d) * rows, rows)
        cot_ref[pl.ds(seat, rows), :] = packs[d][:, half : half + width]
        block = packs[d][:, start : start + 128].astype(F32)[8:16].T[0:rows].astype(BF)
        pos_ref[pl.ds(seat, rows), :] = nn(block, posw)
        lists = packs[d][:, start : start + edges]
        values = lists.astype(F32)[0:8]
        sender = join(values)
        receiver = values[2:3].astype(jnp.int32)
        lanes = slice(d * edges, (d + 1) * edges)
        near_far = shard + (n_mesh - 1) * n_edge * COARSE
        picks_ref[0:shard, lanes] = one_hot(shard, receiver)
        picks_ref[shard : shard + near_far, lanes] = one_hot(near_far, sender)
        picks_ref[shard + near_far : shard + near_far + 16, lanes] = lists
        far = sender - shard
        far_seat = lax.bitwise_and(lax.shift_right_logical(far, shift_of(COARSE)), n_edge - 1)
        far_row = lax.shift_right_logical(far, shift_of(COARSE * n_edge)) * COARSE + lax.bitwise_and(far, COARSE - 1)
        far_row = jnp.where((far >= 0) & (far_seat == e), far_row, -1)
        far_height = far_rows(sizes)
        near_row = jnp.where(far < 0, sender - e * rows, -1)
        spread_ref[0:far_height, lanes] = one_hot(far_height, far_row)
        spread_ref[far_height : far_height + rows, lanes] = one_hot(rows, near_row)
        spread_ref[far_height + rows : far_height + 2 * rows, lanes] = one_hot(rows, receiver - e * rows)
    slope_ref[...] = nt(cot_ref[...], update_ref[...])
    own_ref[...] = packs[0][:, half : half + width]


def far_rows(sizes):
    return -(-(sizes["n_mesh"] - 1) * COARSE // 16) * 16


def node_kernel(sizes, parts_count, *refs):
    n_edge, rows = sizes["n_edge"], sizes["rows"]
    parts, refs = refs[:parts_count], refs[parts_count:]
    enter_ref, pos_ref, second_ref, latent_ref, coarse_ref, coarse_work = refs
    total = parts[0][...].astype(F32)
    for part in parts[1:]:
        total = total + part[...].astype(F32)
    hidden = silu(nn(total.astype(BF), enter_ref[...]) + pos_ref[...]).astype(BF)
    latent = layer_norm(nn(hidden, second_ref[...]))
    latent_ref[...] = latent.astype(BF)
    for d in range(n_edge):
        coarse_work[d * COARSE : (d + 1) * COARSE] = latent[d * rows : d * rows + COARSE]
    coarse_ref[...] = coarse_work[...].astype(BF)


def local_kernel(latent_ref, send_w, recv_w, geom_w, state_w, near_ref, recv_ref, geom_ref, state_ref):
    latent = latent_ref[...]
    near_ref[...] = (0.5 * nn(latent, send_w[...])).astype(BF)
    recv_ref[...] = (0.5 * nn(latent, recv_w[...])).astype(BF)
    geom_ref[...] = geometry_rows(geom_w[...], 16).astype(BF)
    state_ref[...] = nn(latent, state_w[...])


def process_kernel(sizes, *refs):
    n_edge, n_mesh, rows, shard = sizes["n_edge"], sizes["n_mesh"], sizes["rows"], sizes["shard"]
    latent_ref, near_ref, recv_ref, geom_ref, state_ref = refs[:5]
    coarse, refs = refs[5 : 4 + n_mesh], refs[4 + n_mesh :]
    send_w, pass_w, slope_ref, picks_ref, spread_ref, own_ref = refs[:6]
    far_out, refs = refs[6 : 5 + n_mesh], refs[5 + n_mesh :]
    keep_ref, bend_ref, stack_ref, table_ref, back_ref, sum_ref, out_sum_ref = refs
    e = lax.axis_index("edge")
    total = picks_ref.shape[1]
    group = min(1024, total)
    far = jnp.concatenate([c[...] for c in coarse], axis=0)
    products = jnp.concatenate(
        [recv_ref[...], near_ref[...], (0.5 * nn(far, send_w[...])).astype(BF), geom_ref[...]], axis=0
    ).astype(F32).T.astype(BF)
    table_ref[...] = products
    sum_ref[...] = jnp.zeros_like(sum_ref)
    out_sum_ref[...] = jnp.zeros_like(out_sum_ref)

    def forward(k, carry):
        lanes = pl.ds(pl.multiple_of(k * group, group), group)
        half_pre = nn(table_ref[...], picks_ref[:, lanes])
        bend = jnp.tanh(half_pre)
        rise = 1.0 + bend
        act = half_pre * rise
        bend_ref[:, lanes] = rise + act * (1.0 - bend)
        sum_ref[...] += nt(picks_ref[0:shard, lanes], act.astype(BF))
        return carry

    lax.fori_loop(0, total // group, forward, 0)
    act_sum = sum_ref[...]
    update_pre = nn(act_sum.astype(BF), pass_w[...]) + state_ref[...]
    half_update = 0.5 * update_pre
    bend = jnp.tanh(half_update)
    update_act = half_update * (1.0 + bend)
    grad_pre = (slope_ref[...] * (0.5 * (1.0 + bend) * (1.0 + half_update * (1.0 - bend)))).astype(BF)
    grad_act = (0.5 * nt(grad_pre, pass_w[...])).T.astype(BF)
    back_ref[...] = grad_act

    def backward(k, carry):
        lanes = pl.ds(pl.multiple_of(k * group, group), group)
        grad_edge = (nn(back_ref[...], picks_ref[0:shard, lanes]) * bend_ref[:, lanes]).astype(BF)
        out_sum_ref[...] += nt(spread_ref[:, lanes], grad_edge)
        return carry

    lax.fori_loop(0, total // group, backward, 0)
    sums = out_sum_ref[...]
    sums = sums.astype(BF)
    far_height = far_rows(sizes)
    returned = nt(sums[0:far_height], send_w[...])
    for m in range(n_mesh - 1):
        far_out[m][...] = returned[m * COARSE : (m + 1) * COARSE]
    stack_ref[0] = latent_ref[...]
    stack_ref[1] = update_act.astype(BF)
    stack_ref[2] = grad_pre
    seat = pl.multiple_of(e * rows, rows)
    for k in range(3):
        keep_ref[k] = stack_ref[k, pl.ds(seat, rows), :]
    keep_ref[3] = own_ref[...]
    keep_ref[4] = sums[far_height : far_height + rows]
    keep_ref[5] = sums[far_height + rows : far_height + 2 * rows]


def finish_kernel(keep_ref, send_w, recv_w, state_w, update_w, out_ref, base_ref):
    out_ref[...] = (keep_ref[0].astype(F32) + nn(keep_ref[1], update_w[...])).astype(BF)
    base_ref[...] = (
        keep_ref[3].astype(F32)
        + nt(keep_ref[2], state_w[...])
        + nt(keep_ref[4], send_w[...])
        + nt(keep_ref[5], recv_w[...])
    )


def close_kernel(base_ref, *refs):
    returned, out_ref = refs[:-1], refs[-1]
    total = returned[0][...]
    for part in returned[1:]:
        total = total + part[...]
    out_ref[...] = base_ref[...]
    out_ref[0:COARSE] = base_ref[0:COARSE] + total


def call(kernel, name, outs, scratch=(), specs=None, limit=16 << 20):
    def run(*args):
        return pl.pallas_call(
            kernel,
            name=name,
            out_shape=[jax.ShapeDtypeStruct(shape, dtype) for shape, dtype in outs],
            in_specs=specs or [IN_VMEM] * len(args),
            out_specs=[IN_VMEM] * len(outs),
            scratch_shapes=list(scratch),
            compiler_params=pltpu.CompilerParams(vmem_limit_bytes=limit),
        )(*args)

    return run


def in_hbm(value):
    return pltpu.with_memory_space_constraint(value, pltpu.HBM)


def partner(value, axis, size, step):
    return lax.ppermute(value, axis, [(i, i ^ step) for i in range(size)])


def shards(
    grid_input,
    mesh_position,
    encoder_senders,
    encoder_receivers,
    encoder_features,
    encoder_counts,
    mesh_senders,
    mesh_receivers,
    mesh_features,
    cotangent,
    grid_first,
    grid_second,
    encoder_inner,
    encoder_geometry,
    encoder_outer,
    node_first,
    node_position,
    node_second,
    edge_sender,
    edge_receiver,
    edge_geometry,
    edge_outer,
    update_message,
    update_state,
    update_outer,
):
    n_edge, n_mesh = lax.axis_size("edge"), lax.axis_size("mesh")
    own, width = grid_input.shape[0], grid_second.shape[1]
    rows, slots, edges = mesh_position.shape[1], encoder_senders.shape[0], mesh_senders.shape[0]
    shard, half = rows * n_edge, encoder_senders.shape[0] // 2
    assert rows == PERIOD and n_edge & (n_edge - 1) == 0 and n_mesh & (n_mesh - 1) == 0
    sizes = dict(
        n_edge=n_edge, n_mesh=n_mesh, rows=rows, shard=shard, half=half, width=width, edges=edges, band=own * n_edge
    )
    lanes = half + width + edges
    lists = (
        encoder_senders.reshape(1, slots),
        encoder_receivers.reshape(1, slots),
        encoder_features,
        mesh_senders.reshape(1, edges),
        mesh_receivers.reshape(1, edges),
        mesh_features,
        mesh_position,
        cotangent,
    )
    (pack,) = call(
        functools.partial(pack_kernel, sizes),
        "pack",
        [((16, lanes), BF)],
        [pltpu.VMEM((16, lanes), F32)] + [pltpu.VMEM(v.shape, v.dtype) for v in lists] + [pltpu.SemaphoreType.DMA((8,))],
        [IN_SMEM] + [IN_HBM] * 8,
    )(encoder_counts, *[in_hbm(v) for v in lists])
    packs = [pack] + [partner(pack, "edge", n_edge, m) for m in range(1, n_edge)]
    grid_operands = (grid_input.T, grid_first, grid_second, encoder_inner)
    table, geometry = call(
        grid_kernel,
        "grid",
        [((width, own), BF), ((width, 8), BF)],
        [pltpu.VMEM(v.shape, v.dtype) for v in grid_operands] + [pltpu.SemaphoreType.DMA((4,))],
        [IN_VMEM] + [IN_HBM] * 4,
    )(encoder_geometry, *[in_hbm(v) for v in grid_operands])
    places = n_edge * slots // BLOCK + SORT * PAIR
    places = -(-places // 16) * 16
    (partial,) = call(
        functools.partial(encode_kernel, sizes),
        "encode",
        [((shard, width), BF)],
        [
            pltpu.VMEM((places, 8, BLOCK), F32),
            pltpu.VMEM((places, BLOCK), F32),
            pltpu.VMEM((places, BLOCK), jnp.int32),
            pltpu.VMEM((shard, width), F32),
        ],
    )(*packs, table, geometry)
    parts = [partial] + [partner(partial, "edge", n_edge, m) for m in range(1, n_edge)]
    near_far = shard + (n_mesh - 1) * n_edge * COARSE
    heads = shard + near_far + 16
    enter, through, position, slope, picks, spread, own_cot = call(
        functools.partial(prep_kernel, sizes),
        "prep",
        [
            ((width, width), BF),
            ((width, width), BF),
            ((shard, width), F32),
            ((shard, width), F32),
            ((heads, edges * n_edge), BF),
            ((far_rows(sizes) + 2 * rows, edges * n_edge), BF),
            ((rows, width), BF),
        ],
        [pltpu.VMEM((shard, width), BF)],
    )(*packs, partial, node_position, encoder_outer, node_first, edge_outer, update_message, update_outer)
    latent, coarse = call(
        functools.partial(node_kernel, sizes, len(parts)),
        "node",
        [((shard, width), BF), ((n_edge * COARSE, width), BF)],
        [pltpu.VMEM((n_edge * COARSE, width), F32)],
    )(*parts, enter, position, node_second)
    others = [partner(coarse, "mesh", n_mesh, m) for m in range(1, n_mesh)]
    local = call(
        local_kernel,
        "local",
        [((shard, width), BF), ((shard, width), BF), ((16, width), BF), ((shard, width), F32)],
    )(latent, edge_sender, edge_receiver, edge_geometry, update_state)
    *far, keep = call(
        functools.partial(process_kernel, sizes),
        "process",
        [((COARSE, width), F32)] * (n_mesh - 1) + [((6, rows, width), BF)],
        [
            pltpu.VMEM((width, edges * n_edge), F32),
            pltpu.VMEM((3, shard, width), BF),
            pltpu.VMEM((width, heads), BF),
            pltpu.VMEM((width, shard), BF),
            pltpu.VMEM((shard, width), F32),
            pltpu.VMEM((far_rows(sizes) + 2 * rows, width), F32),
        ],
    )(latent, *local, *others, edge_sender, through, slope, picks, spread, own_cot)
    returned = [partner(far[m - 1], "mesh", n_mesh, m) for m in range(1, n_mesh)]
    output, base = call(finish_kernel, "finish", [((rows, width), BF), ((rows, width), F32)])(
        keep, edge_sender, edge_receiver, update_state, update_outer
    )
    (gradient,) = call(close_kernel, "close", [((rows, width), F32)])(base, *returned)
    return (output, gradient)


def solution(mesh):
    nodes = P(("groups", "mesh", "edge"), None)
    flat = P(("mesh", "edge"))
    lanes = P(None, ("mesh", "edge"))
    in_specs = (nodes, lanes, flat, flat, lanes, flat, flat, flat, lanes, nodes) + (P(),) * 15
    return jax.shard_map(shards, mesh=mesh, in_specs=in_specs, out_specs=(nodes, nodes), check_vma=False)
```
